32 devices in a mesh: section: 2 (over y), dp: 4 (over x, core), expert: 4 (over z).
Axes of the slice: x: 2, y: 2, z: 4, core: 2. Of those that a mesh axis runs over, the one named last changes fastest.
Arguments:
- grad_in: bfloat16 [4096, 7168], P(('section', 'dp', 'expert')), may hold values from -4 to 4
- expert_ids: int32 [4096, 2], P(('section', 'dp', 'expert')), may hold values from 0 to 3, all different within a row; in each aligned block of 128 rows (0 to 127, 128 to 255, ...) at most 96 rows name the same one
- gate_probs: float32 [4096, 2], P(('section', 'dp', 'expert')), may hold values from 0.1 to 1
- gate_pre: bfloat16 [2, 4, 4, 384, 1024], P('section', 'dp', 'expert'), may hold values from -5 to 5
- up_pre: bfloat16 [2, 4, 4, 384, 1024], P('section', 'dp', 'expert'), may hold values from -1.5 to 1.5
- w_down: bfloat16 [2, 4, 1024, 7168], P('section', 'expert', None, 'dp'), may hold values from -0.0625 to 0.0625
Outputs:
- gate_grad: bfloat16 [2, 4, 4, 384, 1024], P('section', 'dp', 'expert')
- up_grad: bfloat16 [2, 4, 4, 384, 1024], P('section', 'dp', 'expert')
- down_grad: bfloat16 [2, 4, 7168, 1024], P('section', 'expert', 'dp')
- prob_grad: float32 [4096, 2], P(('section', 'dp', 'expert'))
The draws below stay inside these ranges and needn't reach their ends.
Inputs may be any that keep to these rules, and one draw needn't show every extreme that they name: `expert_ids`: each token names 2 different experts. Among the rows of one device no expert is named by more than 96 rows, and in every draw some expert is named by exactly 96.
All inputs are finite; a program needn't handle non-finite values.
Results may differ from the reference program's by a relative error of at most 0.014.
Values may be sent and summed in bfloat16 or wider, within the bound.
No kernel may reach another device: no remote copies, remote signals or barrier semaphores. Data moves between devices by JAX's collectives and lax.ppermute only.
A program may use at most 128 MiB of HBM per device.

```python
import math
import jax
import jax.numpy as jnp
import numpy as np
from jax import lax

D = 7168
HW = 1024
TOPK = 2
TOK_DEV = 128
EXPERTS = 4
CAP = 96
SLOTS = 384
TOKENS = 4096
N_SECTION = 2
N_DP = 4


def shard_levels(rng, shape, pieces, smallest, high):
    def one(dim, shards_of):
        steps = jax.random.uniform(jax.random.fold_in(jax.random.fold_in(rng, 6), dim), (shards_of,), jnp.float32, smallest / len(pieces), high / len(pieces))
        return jnp.repeat(jnp.exp(steps), shape[dim] // shards_of).reshape((-1,) + (1,) * (len(shape) - dim - 1))

    loudness = one(*pieces[0])
    for cut in pieces[1:]:
        loudness = loudness * one(*cut)
    return loudness


def shared_out(key, own, number, rows, count, top, bound, slope):
    sequence = jax.random.permutation(key, count)
    heavy_load, usual = portions_of(count, rows * top, bound, slope, True), portions_of(count, rows * top, bound, slope, False)
    places = jnp.arange(count)

    def named(sizes, offset_by):
        used = int((sizes > 0).sum())
        fixed = max(1, used // 4)
        passed = fixed + (places - fixed + offset_by * (used - fixed)) % max(1, count - fixed)
        return jnp.zeros((count,), jnp.int32).at[sequence[jnp.where(places < fixed, places, passed)]].set(jnp.asarray(sizes, jnp.int32))

    sizes = jnp.where(number % 4 == 0, named(heavy_load, number // 4), named(usual, number - number // 4 - 1))
    mixed = jax.random.permutation(jax.random.fold_in(own, 3), count)
    source_of, sink = mixed[0:count // 2 * 2:2], mixed[1:count // 2 * 2:2]
    slack = jnp.minimum(sizes[source_of] - 1, bound - sizes[sink]) // 2
    slack = jnp.where((source_of == sequence[0]) | (sink == sequence[0]) | (sizes[sink] == 0), 0, jnp.maximum(slack, 0))
    passed = jax.random.randint(jax.random.fold_in(own, 4), (count // 2,), 0, 1 << 20) % (slack + 1)
    sizes = sizes.at[source_of].add(-passed).at[sink].add(passed)
    members = jnp.searchsorted(jnp.cumsum(sizes), jnp.arange(rows * top), side="right").astype(jnp.int32)
    table = members.reshape(top, rows).T
    table = table[jax.random.permutation(jax.random.fold_in(own, 1), rows)]
    offset_by = jax.random.randint(jax.random.fold_in(own, 2), (rows, 1), 0, top)
    return jnp.take_along_axis(table, (jnp.arange(top)[None, :] + offset_by) % top, axis=1)


def portions_of(count, total, bound, skew, full):
    loads = [(1 << 20) // math.isqrt(standing ** skew) + 1 for standing in range(1, count + 1)]
    largest = bound if full else min(bound, max(-(-total // count), total * loads[0] // sum(loads)))
    least = 1 if total - largest >= count - 1 else 0
    counts, surplus = [largest] + [least] * (count - 1), total - largest - least * (count - 1)
    while surplus > 0:
        movable = [i for i in range(1, count) if counts[i] < largest] or [i for i in range(1, count) if counts[i] < bound]
        pool, remaining = sum([loads[i] for i in movable]), surplus
        for i in movable:
            extra = min(bound - counts[i], max(1, remaining * loads[i] // pool), surplus)
            counts[i] = counts[i] + extra
            surplus = surplus - extra
    return np.array(counts)


def scatter_about(key, dims, scale, bound, shards=(), held_as=jnp.bfloat16):
    level = shard_levels(key, dims, shards, -0.22, 0.18) if shards else 1.0
    values = jax.random.normal(key, dims, jnp.float32) * scale * level
    return jnp.minimum(jnp.maximum(values, -bound), bound).astype(held_as)


def setup_inputs(seed: int = 0) -> dict:
    key_list = jax.random.split(jax.random.key(seed), 7)
    grad_in = scatter_about(key_list[0], (TOKENS, D), 0.5, 4.0, ((0, 32),))
    expert_ids_keys = jax.random.split(jax.random.fold_in(key_list[1], 1), TOKENS // TOK_DEV)
    expert_ids_turns = jax.random.permutation(jax.random.fold_in(key_list[1], 3), TOKENS // TOK_DEV)
    expert_ids = jax.vmap(lambda own, number: shared_out(jax.random.fold_in(key_list[1], 2), own, number, TOK_DEV, EXPERTS, TOPK, CAP, 2))(expert_ids_keys, expert_ids_turns).reshape((TOKENS, TOPK))
    gate_probs = jnp.clip(0.1 + 0.9 * jax.random.uniform(key_list[2], (TOKENS, TOPK), jnp.float32) ** shard_levels(key_list[2], (TOKENS, TOPK), ((0, 32),), -0.2, 0.2), 0.1, 1.0)
    gate_pre = scatter_about(key_list[3], (N_SECTION, N_DP, EXPERTS, SLOTS, HW), 1.0, 5.0, ((0, 2), (1, 4), (2, 4)))
    up_pre = scatter_about(key_list[4], (N_SECTION, N_DP, EXPERTS, SLOTS, HW), 0.25, 1.5, ((0, 2), (1, 4), (2, 4)))
    w_down = scatter_about(key_list[5], (N_SECTION, EXPERTS, HW, D), D ** -0.5, 0.0625, ((0, 2), (1, 4), (3, 4)))
    return {"grad_in": grad_in, "expert_ids": expert_ids, "gate_probs": gate_probs, "gate_pre": gate_pre, "up_pre": up_pre, "w_down": w_down}


def route(expert_rows, groups, capacity):
    flat_ids = expert_rows.reshape(-1)
    onehot_table = (flat_ids[:, None] == jnp.arange(groups, dtype=jnp.int32)[None, :]).astype(jnp.int32)
    earlier = jnp.cumsum(onehot_table, axis=0) - onehot_table
    position = jnp.sum(earlier * onehot_table, axis=1).astype(jnp.int32)
    target = (flat_ids * capacity + position).astype(jnp.int32)
    assigned = flat_ids.shape[0]
    slot_table = jnp.zeros((groups * capacity,), jnp.int32).at[target].set(jnp.arange(assigned, dtype=jnp.int32))
    filled = jnp.zeros((groups * capacity,), jnp.int32).at[target].set(jnp.ones((assigned,), jnp.int32))
    return slot_table, filled, target


def one_expert(inputs):
    grad_rows, prob_rows, gate_rows, up_rows, weights = inputs
    replicas, slots, width = grad_rows.shape
    gate_vals = gate_rows.astype(jnp.float32)
    up_vals = up_rows.astype(jnp.float32)
    sig_gate = jax.nn.sigmoid(gate_vals)
    silu_gate = gate_vals * sig_gate
    hidden = (silu_gate * up_vals).astype(jnp.bfloat16)
    grad_raw = jnp.dot(grad_rows.reshape(replicas * slots, width), weights.T, preferred_element_type=jnp.float32)
    grad_raw = grad_raw.reshape(replicas, slots, -1)
    score = jnp.sum(hidden.astype(jnp.float32) * grad_raw, axis=-1)
    grad_hidden = prob_rows[..., None] * grad_raw
    up_grad = (grad_hidden * silu_gate).astype(jnp.bfloat16)
    gate_grad = (grad_hidden * up_vals * sig_gate * (1.0 + gate_vals * (1.0 - sig_gate))).astype(jnp.bfloat16)
    scaled = (prob_rows[..., None] * grad_rows.astype(jnp.float32)).astype(jnp.bfloat16)
    partial_value = jnp.einsum("rsd,rsh->rdh", scaled.astype(jnp.float32), hidden.astype(jnp.float32)).astype(jnp.bfloat16)
    down_grad = jnp.sum(partial_value.astype(jnp.float32), axis=0).astype(jnp.bfloat16)
    return gate_grad, up_grad, down_grad, score


def reference(grad_in, expert_ids, gate_probs, gate_pre, up_pre, w_down):
    sections, replicas, groups, slots, hidden_width = gate_pre.shape
    capacity = slots // groups
    top_count = expert_ids.shape[1]
    tokens_dev = grad_in.shape[0] // (sections * replicas * groups)
    dmodel = grad_in.shape[1]
    blocks = replicas * groups
    incoming_all = jnp.roll(grad_in.reshape(sections, blocks, tokens_dev, dmodel), -1, axis=0)
    ids_all = expert_ids.reshape(sections, blocks, tokens_dev, top_count)
    probs_all = gate_probs.reshape(sections, blocks, tokens_dev * top_count)

    def one_section(inputs):
        incoming, section_ids, section_probs, gates, ups, weights = inputs
        slot_table, filled, target = jax.vmap(lambda rows: route(rows, groups, capacity))(section_ids)
        token_rows = (slot_table // top_count).astype(jnp.int32)
        picked = jnp.take_along_axis(incoming, token_rows[:, :, None], axis=1)
        send_grad = jnp.where(filled[:, :, None] > 0, picked, jnp.zeros((), jnp.bfloat16))
        send_prob = jnp.where(filled > 0, jnp.take_along_axis(section_probs, slot_table, axis=1), jnp.float32(0.0))
        slot_grad = send_grad.reshape(replicas, groups, groups, capacity, dmodel).transpose(2, 0, 1, 3, 4)
        slot_grad = slot_grad.reshape(groups, replicas, slots, dmodel)
        slot_prob = send_prob.reshape(replicas, groups, groups, capacity).transpose(2, 0, 1, 3).reshape(groups, replicas, slots)
        gate_grad, up_grad, down_grad, score = lax.map(
            one_expert, (slot_grad, slot_prob, gates.transpose(1, 0, 2, 3), ups.transpose(1, 0, 2, 3), weights))
        returned = score.reshape(groups, replicas, groups, capacity).transpose(1, 2, 0, 3).reshape(blocks, groups * capacity)
        prob_grad = jnp.take_along_axis(returned, target, axis=1)
        return gate_grad.transpose(1, 0, 2, 3), up_grad.transpose(1, 0, 2, 3), down_grad, prob_grad

    gate_grad, up_grad, down_grad, prob_grad = lax.map(
        one_section, (incoming_all, ids_all, probs_all, gate_pre, up_pre, w_down))
    return gate_grad, up_grad, down_grad, prob_grad.reshape(-1, top_count)
```

```python
import jax
import jax.numpy as jnp
from jax import lax
from jax.sharding import PartitionSpec as P


def ordered(count):
    rest = [count // 2] + [d for d in range(1, count) if d != count // 2]
    return (rest if count > 1 else []) + [0]


def before(assigned):
    tokens = assigned.shape[-1]
    rows = lax.broadcasted_iota(jnp.int32, (tokens, tokens), 0)
    cols = lax.broadcasted_iota(jnp.int32, (tokens, tokens), 1)
    upper = (rows < cols).astype(jnp.bfloat16)
    flat = assigned.reshape(-1, tokens).astype(jnp.bfloat16)
    out = jnp.dot(flat, upper, preferred_element_type=jnp.float32)
    return out.reshape(assigned.shape)


def slot_mask(assigned, capacity):
    place = before(assigned)
    slot = lax.broadcasted_iota(jnp.int32, (capacity, 1), 0).astype(jnp.float32)
    return (assigned[..., None, :] > 0) & (place[..., None, :] == slot)


def local(grad_in, expert_ids, gate_probs, gate_pre, up_pre, w_down):
    sections = lax.axis_size("section")
    replicas = lax.axis_size("dp")
    groups = lax.axis_size("expert")
    r_me = lax.axis_index("dp")
    e_me = lax.axis_index("expert")
    slots = gate_pre.shape[3]
    capacity = slots // groups
    tokens, top_count = expert_ids.shape
    width = grad_in.shape[1] // replicas
    order = ordered(replicas)

    def over_dp(value, steps):
        pairs = [(r, (r + steps) % replicas) for r in range(replicas)]
        return lax.ppermute(value, "dp", pairs)

    ids = expert_ids.T.astype(jnp.float32)
    info = jnp.concatenate([ids, gate_probs.T], axis=0)
    info = jnp.broadcast_to(info[None], (replicas * groups,) + info.shape)
    info = lax.all_to_all(info, ("dp", "expert"), split_axis=0, concat_axis=0, tiled=True)
    info = info.reshape(replicas, groups, 2 * top_count, tokens)

    blocks = {}
    for d in order:
        pairs = [
            (s * replicas + r, (s - 1) % sections * replicas + (r + d) % replicas)
            for s in range(sections)
            for r in range(replicas)
        ]
        start = (r_me + d) % replicas * width
        piece = lax.dynamic_slice_in_dim(grad_in, start, width, axis=1)
        blocks[d] = lax.ppermute(piece, ("section", "dp"), pairs)

    gate_vals = gate_pre[0, 0, 0].astype(jnp.float32)
    up_vals = up_pre[0, 0, 0].astype(jnp.float32)
    sig_gate = jax.nn.sigmoid(gate_vals)
    silu_gate = gate_vals * sig_gate
    hidden = (silu_gate * up_vals).astype(jnp.bfloat16)
    hiddens = {d: hidden if d == 0 else over_dp(hidden, d) for d in order}

    turn = jnp.arange(replicas)
    at = (r_me - turn) % replicas
    pick = (at[:, None] == turn[None, :]).reshape(replicas, replicas, 1, 1, 1)
    near = jnp.sum(jnp.where(pick, info[None], 0.0), axis=1)
    group = jnp.arange(groups)
    here = (group == e_me).reshape(1, groups, 1, 1)
    mine = jnp.sum(jnp.where(here, near[:, :, :top_count], 0.0), axis=1)

    experts = group.astype(jnp.float32).reshape(1, 1, groups, 1)
    named = jnp.sum((mine[:, :, None, :] == experts).astype(jnp.float32), axis=1)
    select = slot_mask(named, capacity).astype(jnp.bfloat16)
    select = select.reshape(replicas, slots, tokens)

    match = near[:, :, :top_count] == e_me.astype(jnp.float32)
    chosen = jnp.sum(match.astype(jnp.float32), axis=2)
    chance = jnp.sum(jnp.where(match, near[:, :, top_count:], 0.0), axis=2)
    slot_prob = jnp.sum(
        jnp.where(slot_mask(chosen, capacity), chance[:, :, None, :], 0.0), axis=3
    ).reshape(replicas, slots)

    weights = w_down[0, 0]
    total = None
    parts = []
    scores = [None] * replicas
    down = None
    for d in order:
        picked = jnp.dot(select[d], blocks[d], preferred_element_type=jnp.float32).astype(
            jnp.bfloat16
        )
        held = lax.all_to_all(picked, "expert", split_axis=0, concat_axis=0, tiled=True)
        grad_raw = lax.dot_general(
            held, weights, (((1,), (1,)), ((), ())), preferred_element_type=jnp.float32
        )
        scores[d] = jnp.sum(hiddens[d].astype(jnp.float32) * grad_raw, axis=1)
        if d == 0:
            total = grad_raw
        else:
            parts.append(over_dp(grad_raw.astype(jnp.bfloat16), -d))
        weighed = (slot_prob[d][:, None] * hiddens[d].astype(jnp.float32)).astype(jnp.bfloat16)
        term = lax.dot_general(
            held, weighed, (((0,), (0,)), ((), ())), preferred_element_type=jnp.float32
        )
        down = term if down is None else down + term
    for part in parts:
        total = total + part.astype(jnp.float32)

    scores = jnp.stack(scores).reshape(1, replicas, groups, capacity)
    to = (at[None, :] == turn[:, None]).reshape(replicas, replicas, 1, 1)
    scores = jnp.sum(jnp.where(to, scores, 0.0), axis=1)
    scores = scores.reshape(replicas * groups, capacity)
    returned = lax.all_to_all(
        scores, ("dp", "expert"), split_axis=0, concat_axis=0, tiled=True
    ).reshape(replicas, groups, capacity)
    returned = jnp.sum(returned, axis=0)
    hit = ids[:, None, :] == group.astype(jnp.float32)[None, :, None]
    own = slot_mask(jnp.sum(hit.astype(jnp.float32), axis=0), capacity)
    by_expert = jnp.sum(jnp.where(own, returned[:, :, None], 0.0), axis=1)
    prob_grad = jnp.sum(jnp.where(hit, by_expert[None], 0.0), axis=1).T

    grad_hidden = slot_prob[0][:, None] * total
    up_grad = (grad_hidden * silu_gate).astype(jnp.bfloat16)
    gate_grad = (grad_hidden * up_vals * sig_gate * (1.0 + gate_vals * (1.0 - sig_gate))).astype(
        jnp.bfloat16
    )
    return (
        gate_grad.reshape(gate_pre.shape),
        up_grad.reshape(up_pre.shape),
        down.astype(jnp.bfloat16).reshape(1, 1, width, hidden.shape[1]),
        prob_grad,
    )


def solution(mesh):
    in_specs = (
        P(("section", "dp", "expert"), None),
        P(("section", "dp", "expert"), None),
        P(("section", "dp", "expert"), None),
        P("section", "dp", "expert", None, None),
        P("section", "dp", "expert", None, None),
        P("section", "expert", None, "dp"),
    )
    out_specs = (
        P("section", "dp", "expert", None, None),
        P("section", "dp", "expert", None, None),
        P("section", "expert", "dp", None),
        P(("section", "dp", "expert"), None),
    )
    return jax.shard_map(local, mesh=mesh, in_specs=in_specs, out_specs=out_specs, check_vma=False)
```

```python
import jax
import jax.numpy as jnp
from jax import lax
from jax.sharding import PartitionSpec as P


def ordered(count):
    rest = [count // 2] + [d for d in range(1, count) if d != count // 2]
    return (rest if count > 1 else []) + [0]


def before(assigned):
    tokens = assigned.shape[-1]
    rows = lax.broadcasted_iota(jnp.int32, (tokens, tokens), 0)
    cols = lax.broadcasted_iota(jnp.int32, (tokens, tokens), 1)
    upper = (rows < cols).astype(jnp.bfloat16)
    flat = assigned.reshape(-1, tokens).astype(jnp.bfloat16)
    out = jnp.dot(flat, upper, preferred_element_type=jnp.float32)
    return out.reshape(assigned.shape)


def slot_mask(assigned, capacity):
    place = before(assigned)
    slot = lax.broadcasted_iota(jnp.int32, (capacity, 1), 0).astype(jnp.float32)
    return (assigned[..., None, :] > 0) & (place[..., None, :] == slot)


def distances(groups, index):
    if groups != 4:
        return [jnp.full((), k, jnp.int32) for k in range(groups)]
    inner = (index == 1) | (index == 2)
    return [
        index,
        index ^ 1,
        jnp.where(inner, index ^ 3, index ^ 2),
        jnp.where(inner, index ^ 2, index ^ 3),
    ]


def named(ids, expert):
    return jnp.sum((ids == expert).astype(jnp.float32), axis=-2)


def local(grad_in, expert_ids, gate_probs, gate_pre, up_pre, w_down):
    sections = lax.axis_size("section")
    replicas = lax.axis_size("dp")
    groups = lax.axis_size("expert")
    r_me = lax.axis_index("dp")
    e_me = lax.axis_index("expert")
    slots = gate_pre.shape[3]
    capacity = slots // groups
    tokens, top_count = expert_ids.shape
    width = grad_in.shape[1] // replicas
    order = ordered(replicas)
    line = groups == 4

    def over_dp(value, steps):
        pairs = [(r, (r + steps) % replicas) for r in range(replicas)]
        return lax.ppermute(value, "dp", pairs)

    def over_z(value, pairs):
        return lax.ppermute(value, "expert", pairs)

    blocks = {}
    for d in order:
        pairs = [
            (s * replicas + r, (s - 1) % sections * replicas + (r + d) % replicas)
            for s in range(sections)
            for r in range(replicas)
        ]
        start = lax.rem(r_me + d, replicas) * width
        piece = lax.dynamic_slice_in_dim(grad_in, start, width, axis=1)
        blocks[d] = lax.ppermute(piece, ("section", "dp"), pairs)

    ids = expert_ids.T.astype(jnp.float32)
    info = jnp.concatenate([ids, gate_probs.T], axis=0)
    info = jnp.broadcast_to(info[None], (replicas * groups,) + info.shape)
    info = lax.all_to_all(info, ("dp", "expert"), split_axis=0, concat_axis=0, tiled=True)
    info = info.reshape(replicas, groups, 2 * top_count, tokens)

    sources = jnp.stack(distances(groups, e_me))
    turn, group = jnp.arange(replicas), jnp.arange(groups)
    at = lax.rem(r_me - turn + replicas, replicas)
    to_r = at[:, None] == turn[None, :]
    to_j = sources[:, None] == group[None, :]
    pick = to_r[:, None, :, None] & to_j[None, :, None, :]
    near = jnp.sum(jnp.where(pick[..., None, None], info[None, None], 0.0), axis=(2, 3))
    near_ids = near[:, :, :top_count]
    e_val = e_me.astype(jnp.float32)

    gate_vals = gate_pre[0, 0, 0].astype(jnp.float32)
    up_vals = up_pre[0, 0, 0].astype(jnp.float32)
    sig_gate = jax.nn.sigmoid(gate_vals)
    silu_gate = gate_vals * sig_gate
    hidden = (silu_gate * up_vals).astype(jnp.bfloat16)
    if line:
        hidden = hidden.reshape(groups, capacity, -1)
        hidden = jnp.concatenate(
            [lax.dynamic_index_in_dim(hidden, sources[k], 0, False) for k in range(groups)]
        )
    hidden = lax.optimization_barrier(hidden)
    hiddens = {d: hidden if d == 0 else over_dp(hidden, d) for d in order}

    chosen = named(near_ids, e_val)
    match = near_ids == e_val
    chance = jnp.sum(jnp.where(match, near[:, :, top_count:], 0.0), axis=2)
    own_mask = slot_mask(chosen, capacity)
    slot_prob = jnp.sum(jnp.where(own_mask, chance[:, :, None, :], 0.0), axis=3)
    slot_prob = slot_prob.reshape(replicas, slots)

    held = {}
    if line:
        inner = (e_me == 1) | (e_me == 2)
        out_mask = slot_mask(named(near_ids, (e_me ^ 1).astype(jnp.float32)), capacity)
        both = jnp.stack([own_mask, out_mask], axis=2).astype(jnp.bfloat16)
        sent = {}
        middle, inward, outward = [(1, 2), (2, 1)], [(0, 1), (3, 2)], [(1, 0), (2, 3)]

        def picked(d, k, raw, which):
            return jnp.dot(
                both[d, k, which], raw, preferred_element_type=jnp.float32
            ).astype(jnp.bfloat16)

        for d in order:
            block = blocks[d]
            swapped = over_z(block, middle)
            arrived = over_z(block, inward)
            far = over_z(arrived, middle)
            pieces = []
            for k, raw in enumerate((block, arrived, swapped, far)):
                step = {0: 1, 1: 0, 2: 2, 3: 3}[k]
                if step:
                    sent[d, step] = over_z(picked(d, k, raw, 1), outward)
            for k, raw in enumerate((block, arrived, swapped, far)):
                piece = picked(d, k, raw, 0)
                pieces.append(piece if k == 0 else jnp.where(inner, piece, sent[d, k]))
            held[d] = lax.optimization_barrier(jnp.concatenate(pieces))
    else:
        here = (group == e_me).reshape(1, groups, 1, 1)
        mine = jnp.sum(jnp.where(here, near_ids, 0.0), axis=1)
        wanted = named(mine[:, None], group.astype(jnp.float32).reshape(1, groups, 1, 1))
        select = slot_mask(wanted, capacity).astype(jnp.bfloat16).reshape(replicas, slots, tokens)
        for d in order:
            rows = jnp.dot(select[d], blocks[d], preferred_element_type=jnp.float32)
            held[d] = lax.all_to_all(
                rows.astype(jnp.bfloat16), "expert", split_axis=0, concat_axis=0, tiled=True
            )

    weights = w_down[0, 0]
    total = None
    parts = []
    scores = [None] * replicas
    down = None
    for d in order:
        grad_raw = lax.dot_general(
            held[d], weights, (((1,), (1,)), ((), ())), preferred_element_type=jnp.float32
        )
        if d == 0:
            total = grad_raw
        else:
            narrow = grad_raw.astype(jnp.bfloat16)
        scores[d] = jnp.sum(hiddens[d].astype(jnp.float32) * grad_raw, axis=1)
        if d != 0:
            parts.append(over_dp(narrow, -d))
        weighed = (slot_prob[d][:, None] * hiddens[d].astype(jnp.float32)).astype(jnp.bfloat16)
        term = lax.dot_general(
            held[d], weighed, (((0,), (0,)), ((), ())), preferred_element_type=jnp.float32
        )
        down = term if down is None else down + term
        if d != order[-1]:
            down = lax.optimization_barrier(down)
    for part in parts:
        total = total + part.astype(jnp.float32)

    scores = jnp.stack(scores).reshape(replicas, groups, capacity)
    scores = jnp.sum(
        jnp.where(pick[..., None], scores[:, :, None, None, :], 0.0), axis=(0, 1)
    ).reshape(replicas * groups, capacity)
    returned = lax.all_to_all(
        scores, ("dp", "expert"), split_axis=0, concat_axis=0, tiled=True
    ).reshape(replicas, groups, capacity)
    returned = jnp.sum(returned, axis=0)
    hit = ids[:, None, :] == group.astype(jnp.float32)[None, :, None]
    own = slot_mask(jnp.sum(hit.astype(jnp.float32), axis=0), capacity)
    by_expert = jnp.sum(jnp.where(own, returned[:, :, None], 0.0), axis=1)
    prob_grad = jnp.sum(jnp.where(hit, by_expert[None], 0.0), axis=1).T

    grad_hidden = slot_prob[0][:, None] * total
    if line:
        back = jnp.argmax(to_j, axis=0).astype(jnp.int32)
        grad_hidden = grad_hidden.reshape(groups, capacity, -1)
        grad_hidden = jnp.concatenate(
            [lax.dynamic_index_in_dim(grad_hidden, back[j], 0, False) for j in range(groups)]
        )
    up_grad = (grad_hidden * silu_gate).astype(jnp.bfloat16)
    gate_grad = (grad_hidden * up_vals * sig_gate * (1.0 + gate_vals * (1.0 - sig_gate))).astype(
        jnp.bfloat16
    )
    return (
        gate_grad.reshape(gate_pre.shape),
        up_grad.reshape(up_pre.shape),
        down.astype(jnp.bfloat16).reshape(1, 1, width, hidden.shape[1]),
        prob_grad,
    )


def solution(mesh):
    in_specs = (
        P(("section", "dp", "expert"), None),
        P(("section", "dp", "expert"), None),
        P(("section", "dp", "expert"), None),
        P("section", "dp", "expert", None, None),
        P("section", "dp", "expert", None, None),
        P("section", "expert", None, "dp"),
    )
    out_specs = (
        P("section", "dp", "expert", None, None),
        P("section", "dp", "expert", None, None),
        P("section", "expert", "dp", None),
        P(("section", "dp", "expert"), None),
    )

    return jax.shard_map(local, mesh=mesh, in_specs=in_specs, out_specs=out_specs, check_vma=False)
```

```python
import jax
import jax.numpy as jnp
from jax import lax
from jax.experimental import pallas as pl
from jax.experimental.pallas import tpu as pltpu
from jax.sharding import PartitionSpec as P


def ordered(count):
    rest = [count // 2] + [d for d in range(1, count) if d != count // 2]
    return (rest if count > 1 else []) + [0]


def before(assigned):
    tokens = assigned.shape[-1]
    rows = lax.broadcasted_iota(jnp.int32, (tokens, tokens), 0)
    cols = lax.broadcasted_iota(jnp.int32, (tokens, tokens), 1)
    upper = (rows < cols).astype(jnp.bfloat16)
    flat = assigned.reshape(-1, tokens).astype(jnp.bfloat16)
    out = jnp.dot(flat, upper, preferred_element_type=jnp.float32)
    return out.reshape(assigned.shape)


def slot_mask(assigned, capacity):
    place = before(assigned)
    slot = lax.broadcasted_iota(jnp.int32, (capacity, 1), 0).astype(jnp.float32)
    return (assigned[..., None, :] > 0) & (place[..., None, :] == slot)


def tile_of(width):
    return max(t for t in (128, 256, 512, 640, 768, 896) if width % t == 0)


def grad_kernel(last, mask, b0, b1, b2, b3, s1, s2, s3, weights, *refs):
    if last:
        hidden, *parts, held, out, score, total = refs
    else:
        held, out, total = refs
    step = pl.program_id(0)
    capacity = s1.shape[0]
    for k, (block, sent) in enumerate(((b0, None), (b1, s1), (b2, s2), (b3, s3))):
        piece = jnp.dot(mask[k], block[...], preferred_element_type=jnp.float32)
        if sent is not None:
            piece += sent[...].astype(jnp.float32)
        held[k * capacity : (k + 1) * capacity, :] = piece.astype(jnp.bfloat16)
    product = lax.dot_general(
        held[...], weights[...], (((1,), (1,)), ((), ())), preferred_element_type=jnp.float32
    )

    @pl.when(step == 0)
    def _():
        total[...] = product

    @pl.when(step > 0)
    def _():
        total[...] += product

    @pl.when(step == pl.num_programs(0) - 1)
    def _():
        if last:
            value = total[...]
            for part in parts:
                value += part[...].astype(jnp.float32)
            out[...] = value
            score[...] = jnp.sum(hidden[...].astype(jnp.float32) * value, axis=1, keepdims=True)
        else:
            out[...] = total[...].astype(jnp.bfloat16)


def grads(place, masks, raws, sents, weights, extra):
    rows, width = weights.shape
    tokens, capacity = raws[0].shape[0], sents[0].shape[0]
    slots = len(raws) * capacity
    tile = tile_of(width)
    last = extra is not None

    def whole(shape):
        return pl.BlockSpec(shape, lambda i: (0,) * len(shape))

    def columns(height):
        return pl.BlockSpec((height, tile), lambda i: (0, i))

    out_shape = [
        jax.ShapeDtypeStruct((slots, width), jnp.bfloat16),
        jax.ShapeDtypeStruct((slots, rows), jnp.float32 if last else jnp.bfloat16),
    ]
    out_specs = [columns(slots), whole((slots, rows))]
    if last:
        out_shape.append(jax.ShapeDtypeStruct((slots, 1), jnp.float32))
        out_specs.append(whole((slots, 1)))
    call = pl.pallas_call(
        lambda *refs: grad_kernel(last, *refs),
        grid=(width // tile,),
        in_specs=[pl.BlockSpec((None, 4, capacity, tokens), lambda i: (place, 0, 0, 0))]
        + [columns(tokens)] * 4
        + [columns(capacity)] * 3
        + [columns(rows)]
        + [whole((slots, rows))] * (len(extra) if last else 0),
        out_specs=out_specs,
        out_shape=out_shape,
        scratch_shapes=[pltpu.VMEM((slots, rows), jnp.float32)],
        cost_estimate=pl.CostEstimate(
            flops=2 * slots * width * (rows + tokens),
            bytes_accessed=2 * width * (rows + 4 * tokens + 2 * slots) + 4 * slots * rows,
            transcendentals=0,
        ),
    )
    return call(masks, *raws, *sents, weights, *(extra or ()))


def down_kernel(count, *refs):
    held, weighed, out = refs[:count], refs[count : 2 * count], refs[-1]
    value = None
    for rows, factor in zip(held, weighed):
        term = lax.dot_general(
            rows[...], factor[...], (((0,), (0,)), ((), ())), preferred_element_type=jnp.float32
        )
        value = term if value is None else value + term
    out[...] = value.astype(jnp.bfloat16)


def downs(held, weighed):
    slots, width = held[0].shape
    hidden = weighed[0].shape[1]
    tile = 256 if width % 256 == 0 else 128
    count = len(held)
    return pl.pallas_call(
        lambda *refs: down_kernel(count, *refs),
        grid=(width // tile,),
        in_specs=[pl.BlockSpec((slots, tile), lambda i: (0, i))] * count
        + [pl.BlockSpec((slots, hidden), lambda i: (0, 0))] * count,
        out_specs=pl.BlockSpec((tile, hidden), lambda i: (i, 0)),
        out_shape=jax.ShapeDtypeStruct((width, hidden), jnp.bfloat16),
        cost_estimate=pl.CostEstimate(
            flops=2 * count * slots * width * hidden,
            bytes_accessed=2 * (count * slots * (width + hidden) + width * hidden),
            transcendentals=0,
        ),
        name="down",
    )(*held, *weighed)


def distances(groups, index):
    if groups != 4:
        return [jnp.full((), k, jnp.int32) for k in range(groups)]
    inner = (index == 1) | (index == 2)
    return [
        index,
        index ^ 1,
        jnp.where(inner, index ^ 3, index ^ 2),
        jnp.where(inner, index ^ 2, index ^ 3),
    ]


def named(ids, expert):
    return jnp.sum((ids == expert).astype(jnp.float32), axis=-2)


def local(grad_in, expert_ids, gate_probs, gate_pre, up_pre, w_down):
    sections = lax.axis_size("section")
    replicas = lax.axis_size("dp")
    groups = lax.axis_size("expert")
    r_me = lax.axis_index("dp")
    e_me = lax.axis_index("expert")
    slots = gate_pre.shape[3]
    capacity = slots // groups
    tokens, top_count = expert_ids.shape
    width = grad_in.shape[1] // replicas
    order = ordered(replicas)
    line = groups == 4

    def over_dp(value, steps):
        pairs = [(r, (r + steps) % replicas) for r in range(replicas)]
        return lax.ppermute(value, "dp", pairs)

    def over_z(value, pairs):
        return lax.ppermute(value, "expert", pairs)

    blocks = {}
    for d in order:
        pairs = [
            (s * replicas + r, (s - 1) % sections * replicas + (r + d) % replicas)
            for s in range(sections)
            for r in range(replicas)
        ]
        start = lax.rem(r_me + d, replicas) * width
        piece = lax.dynamic_slice_in_dim(grad_in, start, width, axis=1)
        blocks[d] = lax.ppermute(piece, ("section", "dp"), pairs)

    ids = expert_ids.T.astype(jnp.float32)
    info = jnp.concatenate([ids, gate_probs.T], axis=0)
    info = jnp.broadcast_to(info[None], (replicas * groups,) + info.shape)
    info = lax.all_to_all(info, ("dp", "expert"), split_axis=0, concat_axis=0, tiled=True)
    info = info.reshape(replicas, groups, 2 * top_count, tokens)

    sources = jnp.stack(distances(groups, e_me))
    turn, group = jnp.arange(replicas), jnp.arange(groups)
    at = jnp.stack([lax.rem(r_me - d + replicas, replicas) for d in order])
    to_r = at[:, None] == turn[None, :]
    to_j = sources[:, None] == group[None, :]
    pick = to_r[:, None, :, None] & to_j[None, :, None, :]
    near = jnp.sum(jnp.where(pick[..., None, None], info[None, None], 0.0), axis=(2, 3))
    near_ids = near[:, :, :top_count]
    e_val = e_me.astype(jnp.float32)

    gate_vals = gate_pre[0, 0, 0].astype(jnp.float32)
    up_vals = up_pre[0, 0, 0].astype(jnp.float32)
    sig_gate = jax.nn.sigmoid(gate_vals)
    silu_gate = gate_vals * sig_gate
    hidden = (silu_gate * up_vals).astype(jnp.bfloat16)
    if line:
        hidden = hidden.reshape(groups, capacity, -1)
        hidden = jnp.concatenate(
            [lax.dynamic_index_in_dim(hidden, sources[k], 0, False) for k in range(groups)]
        )
    hidden = lax.optimization_barrier(hidden)
    hiddens = {d: hidden if d == 0 else over_dp(hidden, d) for d in order}

    chosen = named(near_ids, e_val)
    match = near_ids == e_val
    chance = jnp.sum(jnp.where(match, near[:, :, top_count:], 0.0), axis=2)
    own_mask = slot_mask(chosen, capacity)
    slot_prob = jnp.sum(jnp.where(own_mask, chance[:, :, None, :], 0.0), axis=3)
    slot_prob = slot_prob.reshape(replicas, slots)

    held = {}
    if line:
        out_mask = slot_mask(named(near_ids, (e_me ^ 1).astype(jnp.float32)), capacity)
        keep, give = own_mask.astype(jnp.bfloat16), out_mask.astype(jnp.bfloat16)
        sent = {}
        middle, inward, outward = [(1, 2), (2, 1)], [(0, 1), (3, 2)], [(1, 0), (2, 3)]

        raws = {}
        for place, d in enumerate(order):
            block = blocks[d]
            arrived = over_z(block, inward)
            swapped = over_z(block, middle)
            far = over_z(arrived, middle)
            raws[d] = (block, arrived, swapped, far)
            for step, k in ((1, 0), (2, 2), (3, 3)):
                some = jnp.dot(
                    give[place, k], raws[d][k], preferred_element_type=jnp.float32
                ).astype(jnp.bfloat16)
                sent[d, step] = over_z(some, outward)
    else:
        here = (group == e_me).reshape(1, groups, 1, 1)
        mine = jnp.sum(jnp.where(here, near_ids, 0.0), axis=1)
        wanted = named(mine[:, None], group.astype(jnp.float32).reshape(1, groups, 1, 1))
        select = slot_mask(wanted, capacity).astype(jnp.bfloat16).reshape(replicas, slots, tokens)
        for place, d in enumerate(order):
            rows = jnp.dot(select[place], blocks[d], preferred_element_type=jnp.float32)
            held[d] = lax.all_to_all(
                rows.astype(jnp.bfloat16), "expert", split_axis=0, concat_axis=0, tiled=True
            )

    weights = w_down[0, 0]
    parts = []
    weighed = []
    for place, d in enumerate(order):
        value = slot_prob[place][:, None] * hiddens[d].astype(jnp.float32)
        weighed.append(value.astype(jnp.bfloat16))
        if line:
            three = [sent[d, step] for step in (1, 2, 3)]
            extra = None if d else [hidden] + parts
            held[d], narrow, *rest = grads(place, keep, raws[d], three, weights, extra)
        else:
            narrow = lax.dot_general(
                held[d], weights, (((1,), (1,)), ((), ())), preferred_element_type=jnp.float32
            )
            if d:
                narrow = narrow.astype(jnp.bfloat16)
        if d:
            parts.append(over_dp(narrow, -d))
        else:
            total = narrow
    if line:
        scores = rest[0]
    else:
        for part in parts:
            total = total + part.astype(jnp.float32)
        scores = jnp.sum(hidden.astype(jnp.float32) * total, axis=1)

    scores = scores.reshape(groups, capacity)
    scores = jnp.sum(jnp.where(to_j[:, :, None], scores[:, None, :], 0.0), axis=0)
    returned = lax.all_to_all(scores, "expert", split_axis=0, concat_axis=0, tiled=True)
    down = downs([held[d] for d in order], weighed)
    hit = ids[:, None, :] == group.astype(jnp.float32)[None, :, None]
    own = slot_mask(jnp.sum(hit.astype(jnp.float32), axis=0), capacity)
    by_expert = jnp.sum(jnp.where(own, returned[:, :, None], 0.0), axis=1)
    prob_grad = jnp.sum(jnp.where(hit, by_expert[None], 0.0), axis=1).T

    grad_hidden = slot_prob[-1][:, None] * total
    if line:
        back = jnp.argmax(to_j, axis=0).astype(jnp.int32)
        grad_hidden = grad_hidden.reshape(groups, capacity, -1)
        grad_hidden = jnp.concatenate(
            [lax.dynamic_index_in_dim(grad_hidden, back[j], 0, False) for j in range(groups)]
        )
    up_grad = (grad_hidden * silu_gate).astype(jnp.bfloat16)
    gate_grad = (grad_hidden * up_vals * sig_gate * (1.0 + gate_vals * (1.0 - sig_gate))).astype(
        jnp.bfloat16
    )
    return (
        gate_grad.reshape(gate_pre.shape),
        up_grad.reshape(up_pre.shape),
        down.reshape(1, 1, width, hidden.shape[1]),
        prob_grad,
    )


def solution(mesh):
    in_specs = (
        P(("section", "dp", "expert"), None),
        P(("section", "dp", "expert"), None),
        P(("section", "dp", "expert"), None),
        P("section", "dp", "expert", None, None),
        P("section", "dp", "expert", None, None),
        P("section", "expert", None, "dp"),
    )
    out_specs = (
        P("section", "dp", "expert", None, None),
        P("section", "dp", "expert", None, None),
        P("section", "expert", "dp", None),
        P(("section", "dp", "expert"), None),
    )

    return jax.shard_map(local, mesh=mesh, in_specs=in_specs, out_specs=out_specs, check_vma=False)
```

```python
import jax
import jax.numpy as jnp
from jax import lax
from jax.experimental import pallas as pl
from jax.experimental.pallas import tpu as pltpu
from jax.sharding import PartitionSpec as P


def ordered(count):
    rest = [count // 2] + [d for d in range(1, count) if d != count // 2]
    return (rest if count > 1 else []) + [0]


def before(assigned):
    tokens = assigned.shape[-1]
    rows = lax.broadcasted_iota(jnp.int32, (tokens, tokens), 0)
    cols = lax.broadcasted_iota(jnp.int32, (tokens, tokens), 1)
    upper = (rows < cols).astype(jnp.bfloat16)
    flat = assigned.reshape(-1, tokens).astype(jnp.bfloat16)
    out = jnp.dot(flat, upper, preferred_element_type=jnp.float32)
    return out.reshape(assigned.shape)


def slot_mask(assigned, capacity):
    place = before(assigned)
    slot = lax.broadcasted_iota(jnp.int32, (capacity, 1), 0).astype(jnp.float32)
    return (assigned[..., None, :] > 0) & (place[..., None, :] == slot)


def tile_of(width):
    return max(t for t in (128, 256, 512, 640, 768, 896) if width % t == 0)


def grad_kernel(mask, b0, b1, b2, b3, s1, s2, s3, weights, held, out, total):
    step = pl.program_id(0)
    capacity = s1.shape[0]
    for k, (block, sent) in enumerate(((b0, None), (b1, s1), (b2, s2), (b3, s3))):
        piece = jnp.dot(mask[k], block[...], preferred_element_type=jnp.float32)
        if sent is not None:
            piece += sent[...].astype(jnp.float32)
        held[k * capacity : (k + 1) * capacity, :] = piece.astype(jnp.bfloat16)
    product = lax.dot_general(
        held[...], weights[...], (((1,), (1,)), ((), ())), preferred_element_type=jnp.float32
    )

    @pl.when(step == 0)
    def _():
        total[...] = product

    @pl.when(step > 0)
    def _():
        total[...] += product

    @pl.when(step == pl.num_programs(0) - 1)
    def _():
        out[...] = total[...].astype(out.dtype)


def grads(place, masks, raws, sents, weights, dtype):
    rows, width = weights.shape
    tokens, capacity = raws[0].shape[0], sents[0].shape[0]
    slots = len(raws) * capacity
    tile = tile_of(width)

    def columns(height):
        return pl.BlockSpec((height, tile), lambda i: (0, i))

    call = pl.pallas_call(
        grad_kernel,
        grid=(width // tile,),
        in_specs=[pl.BlockSpec((None, 4, capacity, tokens), lambda i: (place, 0, 0, 0))]
        + [columns(tokens)] * 4
        + [columns(capacity)] * 3
        + [columns(rows)],
        out_specs=[columns(slots), pl.BlockSpec((slots, rows), lambda i: (0, 0))],
        out_shape=[
            jax.ShapeDtypeStruct((slots, width), jnp.bfloat16),
            jax.ShapeDtypeStruct((slots, rows), dtype),
        ],
        scratch_shapes=[pltpu.VMEM((slots, rows), jnp.float32)],
        cost_estimate=pl.CostEstimate(
            flops=2 * slots * width * (rows + tokens),
            bytes_accessed=2 * width * (rows + 4 * tokens + 2 * slots) + 4 * slots * rows,
            transcendentals=0,
        ),
        compiler_params=pltpu.CompilerParams(vmem_limit_bytes=16 << 20),
    )
    return call(masks, *raws, *sents, weights)


def down_kernel(count, *refs):
    held, weighed, out = refs[:count], refs[count : 2 * count], refs[-1]
    value = None
    for rows, factor in zip(held, weighed):
        term = lax.dot_general(
            rows[...], factor[...], (((0,), (0,)), ((), ())), preferred_element_type=jnp.float32
        )
        value = term if value is None else value + term
    out[...] = value.astype(jnp.bfloat16)


def downs(held, weighed):
    slots, width = held[0].shape
    hidden = weighed[0].shape[1]
    tile = 256 if width % 256 == 0 else 128
    count = len(held)
    return pl.pallas_call(
        lambda *refs: down_kernel(count, *refs),
        grid=(width // tile,),
        in_specs=[pl.BlockSpec((slots, tile), lambda i: (0, i))] * count
        + [pl.BlockSpec((slots, hidden), lambda i: (0, 0))] * count,
        out_specs=pl.BlockSpec((tile, hidden), lambda i: (i, 0)),
        out_shape=jax.ShapeDtypeStruct((width, hidden), jnp.bfloat16),
        cost_estimate=pl.CostEstimate(
            flops=2 * count * slots * width * hidden,
            bytes_accessed=2 * (count * slots * (width + hidden) + width * hidden),
            transcendentals=0,
        ),
        compiler_params=pltpu.CompilerParams(vmem_limit_bytes=16 << 20),
        name="down",
    )(*held, *weighed)


def distances(groups, index):
    if groups != 4:
        return [jnp.full((), k, jnp.int32) for k in range(groups)]
    inner = (index == 1) | (index == 2)
    return [
        index,
        index ^ 1,
        jnp.where(inner, index ^ 3, index ^ 2),
        jnp.where(inner, index ^ 2, index ^ 3),
    ]


def named(ids, expert):
    return jnp.sum((ids == expert).astype(jnp.float32), axis=-2)


def local(grad_in, expert_ids, gate_probs, gate_pre, up_pre, w_down):
    sections = lax.axis_size("section")
    replicas = lax.axis_size("dp")
    groups = lax.axis_size("expert")
    r_me = lax.axis_index("dp")
    e_me = lax.axis_index("expert")
    slots = gate_pre.shape[3]
    capacity = slots // groups
    tokens, top_count = expert_ids.shape
    width = grad_in.shape[1] // replicas
    order = ordered(replicas)
    line = groups == 4

    def over_dp(value, steps):
        pairs = [(r, (r + steps) % replicas) for r in range(replicas)]
        return lax.ppermute(value, "dp", pairs)

    def over_z(value, pairs):
        return lax.ppermute(value, "expert", pairs)

    blocks = {}
    for d in order:
        pairs = [
            (s * replicas + r, (s - 1) % sections * replicas + (r + d) % replicas)
            for s in range(sections)
            for r in range(replicas)
        ]
        start = lax.rem(r_me + d, replicas) * width
        piece = lax.dynamic_slice_in_dim(grad_in, start, width, axis=1)
        blocks[d] = lax.ppermute(piece, ("section", "dp"), pairs)

    ids = expert_ids.T.astype(jnp.float32)
    info = jnp.concatenate([expert_ids.T.astype(jnp.float32), gate_probs.T], axis=0)
    info = jnp.broadcast_to(info[None], (replicas * groups,) + info.shape)
    info = lax.all_to_all(info, ("dp", "expert"), split_axis=0, concat_axis=0, tiled=True)
    info = info.reshape(replicas, groups, 2 * top_count, tokens)

    sources = jnp.stack(distances(groups, e_me))
    turn, group = jnp.arange(replicas), jnp.arange(groups)
    at = jnp.stack([lax.rem(r_me - d + replicas, replicas) for d in order])
    to_r = at[:, None] == turn[None, :]
    to_j = sources[:, None] == group[None, :]
    pick = to_r[:, None, :, None] & to_j[None, :, None, :]
    near = jnp.sum(jnp.where(pick[..., None, None], info[None, None], 0.0), axis=(2, 3))
    near_ids = near[:, :, :top_count]
    e_val = e_me.astype(jnp.float32)

    gate_vals = gate_pre[0, 0, 0].astype(jnp.float32)
    up_vals = up_pre[0, 0, 0].astype(jnp.float32)
    sig_gate = jax.nn.sigmoid(gate_vals)
    silu_gate = gate_vals * sig_gate
    hidden = (silu_gate * up_vals).astype(jnp.bfloat16)
    if line:
        hidden = hidden.reshape(groups, capacity, -1)
        hidden = jnp.concatenate(
            [lax.dynamic_index_in_dim(hidden, sources[k], 0, False) for k in range(groups)]
        )
    hidden = lax.optimization_barrier(hidden)
    hiddens = {d: hidden if d == 0 else over_dp(hidden, d) for d in order}

    chosen = named(near_ids, e_val)
    match = near_ids == e_val
    chance = jnp.sum(jnp.where(match, near[:, :, top_count:], 0.0), axis=2)
    own_mask = slot_mask(chosen, capacity)
    slot_prob = jnp.sum(jnp.where(own_mask, chance[:, :, None, :], 0.0), axis=3)
    slot_prob = slot_prob.reshape(replicas, slots)

    held = {}
    if line:
        out_mask = slot_mask(named(near_ids, (e_me ^ 1).astype(jnp.float32)), capacity)
        keep, give = own_mask.astype(jnp.bfloat16), out_mask.astype(jnp.bfloat16)
        sent = {}
        middle, inward, outward = [(1, 2), (2, 1)], [(0, 1), (3, 2)], [(1, 0), (2, 3)]

        raws = {}
        for place, d in enumerate(order):
            block = blocks[d]
            arrived = over_z(block, inward)
            swapped = over_z(block, middle)
            far = over_z(arrived, middle)
            raws[d] = (block, arrived, swapped, far)
            for step, k in ((1, 0), (2, 2), (3, 3)):
                some = jnp.dot(
                    give[place, k], raws[d][k], preferred_element_type=jnp.float32
                ).astype(jnp.bfloat16)
                sent[d, step] = over_z(some, outward)
    else:
        here = (group == e_me).reshape(1, groups, 1, 1)
        mine = jnp.sum(jnp.where(here, near_ids, 0.0), axis=1)
        wanted = named(mine[:, None], group.astype(jnp.float32).reshape(1, groups, 1, 1))
        select = slot_mask(wanted, capacity).astype(jnp.bfloat16).reshape(replicas, slots, tokens)
        for place, d in enumerate(order):
            rows = jnp.dot(select[place], blocks[d], preferred_element_type=jnp.float32)
            held[d] = lax.all_to_all(
                rows.astype(jnp.bfloat16), "expert", split_axis=0, concat_axis=0, tiled=True
            )

    weights = w_down[0, 0]
    parts = []
    weighed = []
    for place, d in enumerate(order):
        value = slot_prob[place][:, None] * hiddens[d].astype(jnp.float32)
        weighed.append(value.astype(jnp.bfloat16))
        if line:
            three = [sent[d, step] for step in (1, 2, 3)]
            dtype = jnp.bfloat16 if d else jnp.float32
            held[d], narrow = grads(place, keep, raws[d], three, weights, dtype)
        else:
            narrow = lax.dot_general(
                held[d], weights, (((1,), (1,)), ((), ())), preferred_element_type=jnp.float32
            )
            if d:
                narrow = narrow.astype(jnp.bfloat16)
        if d:
            parts.append(over_dp(narrow, -d))
        else:
            total = narrow
    for part in parts:
        total = total + part.astype(jnp.float32)
    scores = jnp.sum(hidden.astype(jnp.float32) * total, axis=1)

    scores = scores.reshape(groups, capacity)
    scores = jnp.sum(jnp.where(to_j[:, :, None], scores[:, None, :], 0.0), axis=0)
    returned = lax.all_to_all(scores, "expert", split_axis=0, concat_axis=0, tiled=True)
    down = downs([held[d] for d in order], weighed)
    hit = ids[:, None, :] == group.astype(jnp.float32)[None, :, None]
    own = slot_mask(jnp.sum(hit.astype(jnp.float32), axis=0), capacity)
    by_expert = jnp.sum(jnp.where(own, returned[:, :, None], 0.0), axis=1)
    prob_grad = jnp.sum(jnp.where(hit, by_expert[None], 0.0), axis=1).T

    grad_hidden = slot_prob[-1][:, None] * total
    if line:
        back = jnp.argmax(to_j, axis=0).astype(jnp.int32)
        grad_hidden = grad_hidden.reshape(groups, capacity, -1)
        grad_hidden = jnp.concatenate(
            [lax.dynamic_index_in_dim(grad_hidden, back[j], 0, False) for j in range(groups)]
        )
    up_grad = (grad_hidden * silu_gate).astype(jnp.bfloat16)
    gate_grad = (grad_hidden * up_vals * sig_gate * (1.0 + gate_vals * (1.0 - sig_gate))).astype(
        jnp.bfloat16
    )
    return (
        gate_grad.reshape(gate_pre.shape),
        up_grad.reshape(up_pre.shape),
        down.reshape(1, 1, width, hidden.shape[1]),
        prob_grad,
    )


def solution(mesh):
    in_specs = (
        P(("section", "dp", "expert"), None),
        P(("section", "dp", "expert"), None),
        P(("section", "dp", "expert"), None),
        P("section", "dp", "expert", None, None),
        P("section", "dp", "expert", None, None),
        P("section", "expert", None, "dp"),
    )
    out_specs = (
        P("section", "dp", "expert", None, None),
        P("section", "dp", "expert", None, None),
        P("section", "expert", "dp", None),
        P(("section", "dp", "expert"), None),
    )

    return jax.shard_map(local, mesh=mesh, in_specs=in_specs, out_specs=out_specs, check_vma=False)
```

```python
import jax
import jax.numpy as jnp
from jax import lax
from jax.experimental import pallas as pl
from jax.experimental.pallas import tpu as pltpu
from jax.sharding import PartitionSpec as P


def ordered(count):
    rest = [count // 2] + [d for d in range(1, count) if d != count // 2]
    return (rest if count > 1 else []) + [0]


def before(assigned):
    tokens = assigned.shape[-1]
    rows = lax.broadcasted_iota(jnp.int32, (tokens, tokens), 0)
    cols = lax.broadcasted_iota(jnp.int32, (tokens, tokens), 1)
    upper = (rows < cols).astype(jnp.bfloat16)
    flat = assigned.reshape(-1, tokens).astype(jnp.bfloat16)
    out = jnp.dot(flat, upper, preferred_element_type=jnp.float32)
    return out.reshape(assigned.shape)


def slot_mask(assigned, capacity):
    place = before(assigned)
    slot = lax.broadcasted_iota(jnp.int32, (capacity, 1), 0).astype(jnp.float32)
    return (assigned[..., None, :] > 0) & (place[..., None, :] == slot)


def tile_of(width):
    return max(t for t in (128, 256, 512, 640, 768, 896) if width % t == 0)


def grad_kernel(
    mask, chance, hidden, b0, b1, b2, b3, s1, s2, s3, weights, held, weighed, out, total
):
    step = pl.program_id(0)
    capacity = s1.shape[0]
    for k, (block, sent) in enumerate(((b0, None), (b1, s1), (b2, s2), (b3, s3))):
        piece = jnp.dot(mask[k], block[...], preferred_element_type=jnp.float32)
        if sent is not None:
            piece += sent[...].astype(jnp.float32)
        held[k * capacity : (k + 1) * capacity, :] = piece.astype(jnp.bfloat16)
    product = lax.dot_general(
        held[...], weights[...], (((1,), (1,)), ((), ())), preferred_element_type=jnp.float32
    )

    @pl.when(step == 0)
    def _():
        total[...] = product
        for k in range(4):
            rows = slice(k * capacity, (k + 1) * capacity)
            each = mask[k].astype(jnp.float32) * chance[k : k + 1, :]
            prob = jnp.sum(each, axis=1, keepdims=True)
            weighed[rows, :] = (prob * hidden[rows, :].astype(jnp.float32)).astype(jnp.bfloat16)

    @pl.when(step > 0)
    def _():
        total[...] += product

    @pl.when(step == pl.num_programs(0) - 1)
    def _():
        out[...] = total[...].astype(out.dtype)


def in_hbm(value):
    return pltpu.with_memory_space_constraint(value, pltpu.HBM)


def grads(place, masks, chance, hidden, raws, sents, weights, dtype):
    rows, width = weights.shape
    tokens, capacity = raws[0].shape[0], sents[0].shape[0]
    slots = len(raws) * capacity
    tile = tile_of(width)

    def columns(height):
        return pl.BlockSpec((height, tile), lambda i: (0, i))

    call = pl.pallas_call(
        grad_kernel,
        grid=(width // tile,),
        in_specs=[
            pl.BlockSpec((None, 4, capacity, tokens), lambda i: (place, 0, 0, 0)),
            pl.BlockSpec((None, 4, tokens), lambda i: (place, 0, 0)),
            pl.BlockSpec((slots, rows), lambda i: (0, 0)),
        ]
        + [columns(tokens)] * 4
        + [columns(capacity)] * 3
        + [columns(rows)],
        out_specs=[columns(slots)] + [pl.BlockSpec((slots, rows), lambda i: (0, 0))] * 2,
        out_shape=[
            pltpu.HBM((slots, width), jnp.bfloat16),
            pltpu.HBM((slots, rows), jnp.bfloat16),
            jax.ShapeDtypeStruct((slots, rows), dtype),
        ],
        scratch_shapes=[pltpu.VMEM((slots, rows), jnp.float32)],
        cost_estimate=pl.CostEstimate(
            flops=2 * slots * width * (rows + tokens),
            bytes_accessed=2 * width * (rows + 4 * tokens + 2 * slots) + 4 * slots * rows,
            transcendentals=0,
        ),
        compiler_params=pltpu.CompilerParams(vmem_limit_bytes=24 << 20),
    )
    return call(masks, chance, hidden, *raws, *sents, in_hbm(weights))


def down_kernel(count, *refs):
    held, weighed, out = refs[:count], refs[count : 2 * count], refs[-1]
    value = None
    for rows, factor in zip(held, weighed):
        term = lax.dot_general(
            rows[...], factor[...], (((0,), (0,)), ((), ())), preferred_element_type=jnp.float32
        )
        value = term if value is None else value + term
    out[...] = value.astype(jnp.bfloat16)


def downs(held, weighed):
    slots, width = held[0].shape
    hidden = weighed[0].shape[1]
    tile = 256 if width % 256 == 0 else 128
    count = len(held)
    return pl.pallas_call(
        lambda *refs: down_kernel(count, *refs),
        grid=(width // tile,),
        in_specs=[pl.BlockSpec((slots, tile), lambda i: (0, i))] * count
        + [pl.BlockSpec((slots, hidden), lambda i: (0, 0), pipeline_mode=pl.Buffered(1))] * count,
        out_specs=pl.BlockSpec((tile, hidden), lambda i: (i, 0)),
        out_shape=jax.ShapeDtypeStruct((width, hidden), jnp.bfloat16),
        cost_estimate=pl.CostEstimate(
            flops=2 * count * slots * width * hidden,
            bytes_accessed=2 * (count * slots * (width + hidden) + width * hidden),
            transcendentals=0,
        ),
        compiler_params=pltpu.CompilerParams(vmem_limit_bytes=12 << 20),
        name="down",
    )(*map(in_hbm, held), *map(in_hbm, weighed))


def distances(groups, index):
    if groups != 4:
        return [jnp.full((), k, jnp.int32) for k in range(groups)]
    inner = (index == 1) | (index == 2)
    return [
        index,
        index ^ 1,
        jnp.where(inner, index ^ 3, index ^ 2),
        jnp.where(inner, index ^ 2, index ^ 3),
    ]


def named(ids, expert):
    return jnp.sum((ids == expert).astype(jnp.float32), axis=-2)


def local(grad_in, expert_ids, gate_probs, gate_pre, up_pre, w_down):
    sections = lax.axis_size("section")
    replicas = lax.axis_size("dp")
    groups = lax.axis_size("expert")
    r_me = lax.axis_index("dp")
    e_me = lax.axis_index("expert")
    slots = gate_pre.shape[3]
    capacity = slots // groups
    tokens, top_count = expert_ids.shape
    width = grad_in.shape[1] // replicas
    order = ordered(replicas)
    line = groups == 4

    def over_dp(value, steps):
        pairs = [(r, (r + steps) % replicas) for r in range(replicas)]
        return lax.ppermute(value, "dp", pairs)

    def over_z(value, pairs):
        return lax.ppermute(value, "expert", pairs)

    blocks = {}
    for d in order:
        pairs = [
            (s * replicas + r, (s - 1) % sections * replicas + (r + d) % replicas)
            for s in range(sections)
            for r in range(replicas)
        ]
        start = lax.rem(r_me + d, replicas) * width
        piece = lax.dynamic_slice_in_dim(grad_in, start, width, axis=1)
        blocks[d] = lax.ppermute(piece, ("section", "dp"), pairs)

    ids = expert_ids.T.astype(jnp.float32)
    info = jnp.concatenate([expert_ids.T.astype(jnp.float32), gate_probs.T], axis=0)
    info = jnp.broadcast_to(info[None], (replicas * groups,) + info.shape)
    info = lax.all_to_all(info, ("dp", "expert"), split_axis=0, concat_axis=0, tiled=True)
    info = info.reshape(replicas, groups, 2 * top_count, tokens)

    sources = jnp.stack(distances(groups, e_me))
    turn, group = jnp.arange(replicas), jnp.arange(groups)
    at = jnp.stack([lax.rem(r_me - d + replicas, replicas) for d in order])
    to_r = at[:, None] == turn[None, :]
    to_j = sources[:, None] == group[None, :]
    pick = to_r[:, None, :, None] & to_j[None, :, None, :]
    near = jnp.sum(jnp.where(pick[..., None, None], info[None, None], 0.0), axis=(2, 3))
    near_ids = near[:, :, :top_count]
    e_val = e_me.astype(jnp.float32)

    gate_vals = gate_pre[0, 0, 0].astype(jnp.float32)
    up_vals = up_pre[0, 0, 0].astype(jnp.float32)
    sig_gate = jax.nn.sigmoid(gate_vals)
    silu_gate = gate_vals * sig_gate
    hidden = (silu_gate * up_vals).astype(jnp.bfloat16)
    if line:
        hidden = hidden.reshape(groups, capacity, -1)
        hidden = jnp.concatenate(
            [lax.dynamic_index_in_dim(hidden, sources[k], 0, False) for k in range(groups)]
        )
    hidden = lax.optimization_barrier(hidden)
    hiddens = {d: hidden if d == 0 else over_dp(hidden, d) for d in order}

    chosen = named(near_ids, e_val)
    match = near_ids == e_val
    chance = jnp.sum(jnp.where(match, near[:, :, top_count:], 0.0), axis=2)
    own_mask = slot_mask(chosen, capacity)
    slot_prob = jnp.sum(jnp.where(own_mask, chance[:, :, None, :], 0.0), axis=3)
    slot_prob = slot_prob.reshape(replicas, slots)

    held = {}
    if line:
        out_mask = slot_mask(named(near_ids, (e_me ^ 1).astype(jnp.float32)), capacity)
        keep, give = own_mask.astype(jnp.bfloat16), out_mask.astype(jnp.bfloat16)
        sent = {}
        middle, inward, outward = [(1, 2), (2, 1)], [(0, 1), (3, 2)], [(1, 0), (2, 3)]

        raws = {}
        for place, d in enumerate(order):
            block = blocks[d]
            arrived = over_z(block, inward)
            swapped = over_z(block, middle)
            far = over_z(arrived, middle)
            raws[d] = (block, arrived, swapped, far)
            for step, k in ((1, 0), (2, 2), (3, 3)):
                some = jnp.dot(
                    give[place, k], raws[d][k], preferred_element_type=jnp.float32
                ).astype(jnp.bfloat16)
                sent[d, step] = over_z(some, outward)
    else:
        here = (group == e_me).reshape(1, groups, 1, 1)
        mine = jnp.sum(jnp.where(here, near_ids, 0.0), axis=1)
        wanted = named(mine[:, None], group.astype(jnp.float32).reshape(1, groups, 1, 1))
        select = slot_mask(wanted, capacity).astype(jnp.bfloat16).reshape(replicas, slots, tokens)
        for place, d in enumerate(order):
            rows = jnp.dot(select[place], blocks[d], preferred_element_type=jnp.float32)
            held[d] = lax.all_to_all(
                rows.astype(jnp.bfloat16), "expert", split_axis=0, concat_axis=0, tiled=True
            )

    weights = w_down[0, 0]
    parts = []
    weighed = []
    for place, d in enumerate(order):
        if not line:
            value = slot_prob[place][:, None] * hiddens[d].astype(jnp.float32)
            weighed.append(value.astype(jnp.bfloat16))
        if line:
            three = [sent[d, step] for step in (1, 2, 3)]
            dtype = jnp.bfloat16 if d else jnp.float32
            held[d], value, narrow = grads(
                place, keep, chance, hiddens[d], raws[d], three, weights, dtype
            )
            weighed.append(value)
        else:
            narrow = lax.dot_general(
                held[d], weights, (((1,), (1,)), ((), ())), preferred_element_type=jnp.float32
            )
            if d:
                narrow = narrow.astype(jnp.bfloat16)
        if d:
            parts.append(over_dp(narrow, -d))
        else:
            total = narrow
    for part in parts:
        total = total + part.astype(jnp.float32)
    scores = jnp.sum(hidden.astype(jnp.float32) * total, axis=1)

    scores = scores.reshape(groups, capacity)
    scores = jnp.sum(jnp.where(to_j[:, :, None], scores[:, None, :], 0.0), axis=0)
    returned = lax.all_to_all(scores, "expert", split_axis=0, concat_axis=0, tiled=True)
    down = downs([held[d] for d in order], weighed)
    hit = ids[:, None, :] == group.astype(jnp.float32)[None, :, None]
    own = slot_mask(jnp.sum(hit.astype(jnp.float32), axis=0), capacity)
    by_expert = jnp.sum(jnp.where(own, returned[:, :, None], 0.0), axis=1)
    prob_grad = jnp.sum(jnp.where(hit, by_expert[None], 0.0), axis=1).T

    grad_hidden = slot_prob[-1][:, None] * total
    if line:
        back = jnp.argmax(to_j, axis=0).astype(jnp.int32)
        grad_hidden = grad_hidden.reshape(groups, capacity, -1)
        grad_hidden = jnp.concatenate(
            [lax.dynamic_index_in_dim(grad_hidden, back[j], 0, False) for j in range(groups)]
        )
    up_grad = (grad_hidden * silu_gate).astype(jnp.bfloat16)
    gate_grad = (grad_hidden * up_vals * sig_gate * (1.0 + gate_vals * (1.0 - sig_gate))).astype(
        jnp.bfloat16
    )
    return (
        gate_grad.reshape(gate_pre.shape),
        up_grad.reshape(up_pre.shape),
        down.reshape(1, 1, width, hidden.shape[1]),
        prob_grad,
    )


def solution(mesh):
    in_specs = (
        P(("section", "dp", "expert"), None),
        P(("section", "dp", "expert"), None),
        P(("section", "dp", "expert"), None),
        P("section", "dp", "expert", None, None),
        P("section", "dp", "expert", None, None),
        P("section", "expert", None, "dp"),
    )
    out_specs = (
        P("section", "dp", "expert", None, None),
        P("section", "dp", "expert", None, None),
        P("section", "expert", "dp", None),
        P(("section", "dp", "expert"), None),
    )

    return jax.shard_map(local, mesh=mesh, in_specs=in_specs, out_specs=out_specs, check_vma=False)
```
